32 devices in a mesh: dp: 8 (over y, x, core), tensor: 4 (over z).
Axes of the slice: x: 2, y: 2, z: 4, core: 2. Of those that a mesh axis runs over, the one named last changes fastest.
Arguments:
- inputs: bfloat16 [8, 2048, 768], P('dp', 'tensor'), may hold values from -6 to 6
- encoder_out: bfloat16 [8, 1024, 768], P('dp', 'tensor'), may hold values from -6 to 6
- block_ids: int32 [8, 8], P('dp'), may hold values from 0 to 4, never falling along the last dimension, each value on 1 to 3 neighbouring positions
- out_grad: bfloat16 [8, 2048, 768], P('dp', 'tensor'), may hold values from -6 to 6
- in_weight: float32 [6, 768, 768], P(None, 'dp', 'tensor'), may hold values from -0.21875 to 0.21875
- out_weight: float32 [2, 768, 768], P(None, 'tensor', 'dp'), may hold values from -4.8 to 4.8
- up_weight: float32 [768, 3072], P('dp', 'tensor'), may hold values from -0.21875 to 0.21875
- down_weight: float32 [3072, 768], P('tensor', 'dp'), may hold values from -0.109375 to 0.109375
- vectors: float32 [10, 768], replicated, may hold values from -0.24 to 0.24
- norm_gains: float32 [3, 768], replicated, may hold values from 0.25 to 1.75
- up_bias: float32 [3072], replicated, may hold values from -1.8 to 1.8
Outputs:
- layer_out: bfloat16 [8, 2048, 768], P('dp', 'tensor')
- grad_input: float32 [8, 2048, 768], P('dp', 'tensor')
- grad_encoder: float32 [8, 1024, 768], P('dp', 'tensor')
- grad_in_weight: float32 [6, 768, 768], P(None, 'dp', 'tensor')
- grad_out_weight: float32 [2, 768, 768], P(None, 'tensor', 'dp')
- grad_up_weight: float32 [768, 3072], P('dp', 'tensor')
- grad_down_weight: float32 [3072, 768], P('tensor', 'dp')
- grad_vectors: float32 [10, 768], replicated
- grad_gains: float32 [3, 768], replicated
- grad_up_bias: float32 [3072], replicated
The draws below stay inside these ranges and needn't reach their ends.
Inputs may be any that keep to these rules, and one draw needn't show every extreme that they name: `block_ids`: along each sequence the index never falls from one block to the next, and every value from 0 to 4 appears.
All inputs are finite; a program needn't handle non-finite values.
Results may differ from the reference program's by a relative error of at most 0.035.
Values may be sent and summed in bfloat16 or wider, within the bound.
No kernel may reach another device: no remote copies, remote signals or barrier semaphores. Data moves between devices by JAX's collectives and lax.ppermute only.
A program may use at most 128 MiB of HBM per device.

```python
import math
import jax
import jax.numpy as jnp
import numpy as np
from jax import lax

D = 768
H = 12
HD = 64
FF = 3072
SEQ_LEN = 2048
ENC = 1024
BLOCK = 256
NB = 8
SEQS = 8


def level_of(rng, shape, pieces, low, top_value):
    def one(axis_at, shards_of):
        steps = jax.random.uniform(jax.random.fold_in(jax.random.fold_in(rng, 6), axis_at), (shards_of,), jnp.float32, low / len(pieces), top_value / len(pieces))
        return jnp.repeat(jnp.exp(steps), shape[axis_at] // shards_of).reshape((-1,) + (1,) * (len(shape) - axis_at - 1))

    factor_of = one(*pieces[0])
    for cut in pieces[1:]:
        factor_of = factor_of * one(*cut)
    return factor_of


def length_profile(amount, total, reach, lean):
    weights = [(1 << 20) // math.isqrt(standing ** lean) + 1 for standing in range(2, amount + 1)]
    spare, given = total - reach - (amount - 1), [1] * (amount - 1)
    while spare > 0:
        candidates = [i for i in range(amount - 1) if given[i] < reach]
        mass, left = sum([weights[i] for i in candidates]), spare
        for i in candidates:
            more = min(reach - given[i], max(1, left * weights[i] // mass), spare)
            given[i] = given[i] + more
            spare = spare - more
    return np.array([reach] + given)


def ragged_sizes(key, count, total, reach, lean):
    if count == 2:
        one = jax.random.randint(key, (), max(1, total - reach), min(reach, total - 1) + 1)
        return jnp.stack([one, total - one])
    lengths = jnp.asarray(length_profile(count, total, reach, lean), jnp.int32)
    pairs = (count - 1) // 2
    giver, taker = lengths[1:1 + 2 * pairs:2], lengths[2:2 + 2 * pairs:2]
    room = jnp.minimum(giver - 1, reach - taker)
    passed = jax.random.randint(jax.random.fold_in(key, 1), (pairs,), 0, 1 << 20) % (room + 1)
    lengths = lengths.at[1:1 + 2 * pairs:2].set(giver - passed).at[2:2 + 2 * pairs:2].set(taker + passed)
    return lengths[jax.random.permutation(jax.random.fold_in(key, 2), count)]


def centred(own_key, extent, width, reach, shards=(), dtype=jnp.bfloat16):
    drawn = jax.random.normal(own_key, extent, jnp.float32) * width
    if len(shards) > 0:
        drawn = level_of(own_key, extent, shards, -0.22, 0.18) * drawn
    return jnp.clip(drawn, min=-reach, max=reach).astype(dtype)


def setup_inputs(seed: int = 0) -> dict:
    splits = jax.random.split(jax.random.key(seed), 12)
    return {
        "inputs": centred(splits[0], (SEQS, SEQ_LEN, D), 1.0, 6.0, ((0, 8), (1, 4))),
        "encoder_out": centred(splits[1], (SEQS, ENC, D), 1.0, 6.0, ((0, 8), (1, 4))),
        "block_ids": jax.vmap(lambda own: jnp.searchsorted(jnp.cumsum(ragged_sizes(own, NB // 2 + 1, NB, max(2, NB // 2 - 1), 1)), jnp.arange(NB), side="right"))(jax.random.split(splits[2], SEQS)).reshape((SEQS, NB)).astype(jnp.int32),
        "out_grad": centred(splits[3], (SEQS, SEQ_LEN, D), 1.0, 6.0, ((0, 8), (1, 4))),
        "in_weight": centred(splits[4], (6, D, D), D ** -0.5, 0.21875, ((1, 8), (2, 4)), jnp.float32),
        "out_weight": centred(splits[5], (2, D, D), 0.8, 4.8, ((1, 4), (2, 8)), jnp.float32),
        "up_weight": centred(splits[6], (D, FF), D ** -0.5, 0.21875, ((0, 8), (1, 4)), jnp.float32),
        "down_weight": centred(splits[7], (FF, D), FF ** -0.5, 0.109375, ((0, 4), (1, 8)), jnp.float32),
        "vectors": centred(splits[8], (10, D), 0.04, 0.24, (), jnp.float32),
        "norm_gains": jnp.clip(1.0 + 0.15 * jax.random.normal(splits[9], (3, D), jnp.float32), 0.25, 1.75),
        "up_bias": centred(splits[10], (FF,), 0.3, 1.8, (), jnp.float32),
    }


@jax.custom_vjp
def low(v):
    return lax.optimization_barrier(v.astype(jnp.bfloat16)).astype(jnp.float32)

@jax.custom_vjp
def low_back(v):
    return v

def low_keep(v):
    return (low(v), None)

def low_pass(kept, grad):
    return (grad,)

def back_keep(v):
    return (v, None)

def back_low(kept, grad):
    return (low(grad),)
low.defvjp(low_keep, low_pass)
low_back.defvjp(back_keep, back_low)
masked_value = -1e+30
norm_epsilon = 1e-05

def rounded(value):
    return low(low_back(value))

def matmul(former, latter):
    return jnp.dot(former, latter, precision=lax.Precision.HIGHEST)

def layer_norm(summed, norm_gain, norm_shift):
    centered = summed - lax.optimization_barrier(jnp.mean(summed, axis=-1, keepdims=True))
    variance = lax.optimization_barrier(jnp.mean(centered * centered, axis=-1, keepdims=True))
    return centered * lax.rsqrt(variance + norm_epsilon) * norm_gain + norm_shift

def attention(queries, keys_all, values_all, query_ids, key_ids):
    row_count = queries.shape[0]
    block_rows = min(512, row_count)
    block_count = row_count // block_rows
    heads_q = queries.reshape(block_count, block_rows, H, HD)
    heads_k = keys_all.reshape(-1, H, HD)
    heads_v = values_all.reshape(-1, H, HD)
    ids_q = query_ids.reshape(block_count, block_rows)

    def one_block(packed):
        query_block, ids_block = packed
        scores = low_back(jnp.einsum('qhd,khd->hqk', query_block, heads_k, precision=lax.Precision.HIGHEST))
        allowed = key_ids[None, :] <= ids_block[:, None]
        scores = jnp.where(allowed[None], scores, masked_value)
        row_max = lax.optimization_barrier(jnp.max(scores, axis=-1, keepdims=True))
        exponent = jnp.exp(scores - row_max)
        chances = exponent / lax.optimization_barrier(jnp.sum(exponent, axis=-1, keepdims=True))
        return jnp.einsum('hqk,khd->qhd', low(chances), heads_v, precision=lax.Precision.HIGHEST)
    mixed_heads = lax.map(jax.checkpoint(one_block), (heads_q, ids_q))
    return rounded(mixed_heads.reshape(row_count, D))

def one_sequence(tokens, encoded, ids, in_low, out_low, up_low, down_low, vectors, norm_gains, up_bias):
    query_scale = HD ** (-0.5)
    row_ids = jnp.repeat(ids, BLOCK)
    zero_rows = jnp.zeros((SEQ_LEN,), jnp.int32)
    zero_keys = jnp.zeros((ENC,), jnp.int32)
    hidden_self = low(tokens)
    query_self = rounded((matmul(hidden_self, in_low[0]) + vectors[0]) * query_scale)
    key_self = rounded(matmul(hidden_self, in_low[1]))
    value_self = rounded(matmul(hidden_self, in_low[2]) + vectors[1])
    mixed_self = attention(query_self, key_self, value_self, row_ids, row_ids)
    summed_one = tokens + low_back(matmul(mixed_self, out_low[0]) + vectors[4])
    normed_one = layer_norm(summed_one, norm_gains[0], vectors[7])
    hidden_cross = low(normed_one)
    encoder_low = low(encoded)
    query_cross = rounded((matmul(hidden_cross, in_low[3]) + vectors[2]) * query_scale)
    key_cross = rounded(matmul(encoder_low, in_low[4]))
    value_cross = rounded(matmul(encoder_low, in_low[5]) + vectors[3])
    mixed_cross = attention(query_cross, key_cross, value_cross, zero_rows, zero_keys)
    summed_two = normed_one + low_back(matmul(mixed_cross, out_low[1]) + vectors[5])
    normed_two = layer_norm(summed_two, norm_gains[1], vectors[8])
    hidden_ffn = low(normed_two)
    before = low_back(matmul(hidden_ffn, up_low) + up_bias)
    active = low(jax.nn.gelu(before, approximate=False))
    summed_three = normed_two + low_back(matmul(active, down_low) + vectors[6])
    return layer_norm(summed_three, norm_gains[2], vectors[9])

def forward_all(inputs, encoder_out, in_weight, out_weight, up_weight, down_weight, vectors, norm_gains, up_bias, block_ids):
    in_low = low(in_weight)
    out_low = low(out_weight)
    up_low = low(up_weight)
    down_low = low(down_weight)

    def per_sequence(carried, packed):
        tokens, encoded, ids = packed
        result = one_sequence(tokens, encoded, ids, in_low, out_low, up_low, down_low, vectors, norm_gains, up_bias)
        return (carried, result)
    _, outputs = lax.scan(per_sequence, jnp.zeros((), jnp.float32), (inputs, encoder_out, block_ids))
    return outputs

def reference(inputs, encoder_out, block_ids, out_grad, in_weight, out_weight, up_weight, down_weight, vectors, norm_gains, up_bias):

    def forward(tokens, encoded, weight_in, weight_out, weight_up, weight_down, vector_rows, gain_rows, unit_bias):
        return forward_all(tokens, encoded, weight_in, weight_out, weight_up, weight_down, vector_rows, gain_rows, unit_bias, block_ids)
    layer_out, pullback = jax.vjp(forward, inputs.astype(jnp.float32), encoder_out.astype(jnp.float32), in_weight, out_weight, up_weight, down_weight, vectors, norm_gains, up_bias)
    gradients = pullback(out_grad.astype(jnp.float32))
    return (layer_out.astype(jnp.bfloat16), gradients[0], gradients[1], gradients[2], gradients[3], gradients[4], gradients[5], gradients[6], gradients[7], gradients[8])
```

```python
import functools
import jax, jax.numpy as jnp
from jax import lax
from jax.experimental import pallas as pl
from jax.experimental.pallas import tpu as pltpu
HD=64
KB=256
def dot_nn(a,b): return jnp.dot(a,b,preferred_element_type=jnp.float32)
def dot_nt(a,b): return lax.dot_general(a,b,(((1,),(1,)),((),())),preferred_element_type=jnp.float32)

def head_masked(block, h):
    rows = lax.broadcasted_iota(jnp.int32, block.shape, 0)
    return jnp.where((rows >= h*HD) & (rows < (h+1)*HD), block, jnp.zeros_like(block))

def attend_kernel(counts_ref, q_ref, k_ref, v_ref, o_ref, lse_ref, vt_ref, *, heads):
    i = pl.program_id(0)
    nk = k_ref.shape[0]//KB
    bq = q_ref.shape[1]
    @pl.when(i == 0)
    def _():
        for j in range(nk):
            vt_ref[:, j*KB:(j+1)*KB] = v_ref[j*KB:(j+1)*KB, :].T
    q = q_ref[...]
    qm = [head_masked(q, h) for h in range(heads)]
    def step(j, carry):
        start = pl.multiple_of(j*KB, KB)
        kj = k_ref[pl.ds(start, KB), :]
        new = []
        for h in range(heads):
            m, l, acc = carry[h]
            s = dot_nn(kj, qm[h])
            m_new = jnp.maximum(m, jnp.max(s, axis=0, keepdims=True))
            p = jnp.exp(s - m_new)
            alpha = jnp.exp(m - m_new)
            l = l*alpha + jnp.sum(p, axis=0, keepdims=True)
            vt = vt_ref[h*HD:(h+1)*HD, pl.ds(start, KB)]
            acc = acc*alpha + dot_nn(vt, p.astype(jnp.bfloat16))
            new.append((m_new, l, acc))
        return tuple(new)
    init = tuple((jnp.full((1,bq),-1e30,jnp.float32), jnp.zeros((1,bq),jnp.float32), jnp.zeros((HD,bq),jnp.float32)) for _ in range(heads))
    fin = lax.fori_loop(0, counts_ref[i], step, init)
    for h in range(heads):
        m, l, acc = fin[h]
        o_ref[h*HD:(h+1)*HD, :] = (acc/l).astype(jnp.bfloat16)
        lse_ref[h:h+1, :] = m + jnp.log(l)

def attend(counts, q_t, k, v, bq=256):
    width, rows = q_t.shape
    nk = k.shape[0]
    heads = width//HD
    return pl.pallas_call(
        functools.partial(attend_kernel, heads=heads),
        grid_spec=pltpu.PrefetchScalarGridSpec(
            num_scalar_prefetch=1, grid=(rows//bq,),
            in_specs=[pl.BlockSpec((width,bq), lambda i,c:(0,i)),
                      pl.BlockSpec((nk,width), lambda i,c:(0,0)),
                      pl.BlockSpec((nk,width), lambda i,c:(0,0))],
            out_specs=[pl.BlockSpec((width,bq), lambda i,c:(0,i)),
                       pl.BlockSpec((8,bq), lambda i,c:(0,i))],
            scratch_shapes=[pltpu.VMEM((width,nk), jnp.bfloat16)]),
        out_shape=(jax.ShapeDtypeStruct((width,rows),jnp.bfloat16), jax.ShapeDtypeStruct((8,rows),jnp.float32)),
        compiler_params=pltpu.CompilerParams(dimension_semantics=("arbitrary",), vmem_limit_bytes=40<<20),
        name="attend",
    )(counts, q_t, k, v)

def attend_back_kernel(counts_ref, q_ref, g_ref, o_ref, lse_ref, k_ref, v_ref, dq_ref, dkv_ref, kt_ref, dka_ref, dva_ref, *, heads):
    i = pl.program_id(0)
    nk = k_ref.shape[0]//KB
    bq = q_ref.shape[1]
    @pl.when(i == 0)
    def _():
        for j in range(nk):
            kt_ref[:, j*KB:(j+1)*KB] = k_ref[j*KB:(j+1)*KB, :].T
        dka_ref[...] = jnp.zeros_like(dka_ref)
        dva_ref[...] = jnp.zeros_like(dva_ref)
    q = q_ref[...]
    g = g_ref[...]
    prod = g.astype(jnp.float32)*o_ref[...].astype(jnp.float32)
    qm = [head_masked(q, h) for h in range(heads)]
    gm = [head_masked(g, h) for h in range(heads)]
    delta = [jnp.sum(prod[h*HD:(h+1)*HD], axis=0, keepdims=True) for h in range(heads)]
    lse = [lse_ref[h:h+1, :] for h in range(heads)]
    def step(j, carry):
        start = pl.multiple_of(j*KB, KB)
        kj = k_ref[pl.ds(start, KB), :]
        vj = v_ref[pl.ds(start, KB), :]
        new = []
        for h in range(heads):
            lo, hi = h*HD, (h+1)*HD
            p = jnp.exp(dot_nn(kj, qm[h]) - lse[h])
            dp = dot_nn(vj, gm[h])
            ds = (p*(dp - delta[h])).astype(jnp.bfloat16)
            dva_ref[lo:hi, pl.ds(start, KB)] += dot_nt(g[lo:hi], p.astype(jnp.bfloat16))
            dka_ref[lo:hi, pl.ds(start, KB)] += dot_nt(q[lo:hi], ds)
            new.append(carry[h] + dot_nn(kt_ref[lo:hi, pl.ds(start, KB)], ds))
        return tuple(new)
    fin = lax.fori_loop(0, counts_ref[i], step, tuple(jnp.zeros((HD,bq),jnp.float32) for _ in range(heads)))
    for h in range(heads):
        dq_ref[h*HD:(h+1)*HD, :] = (fin[h] * HD**-0.5).astype(jnp.bfloat16)
    @pl.when(i == pl.num_programs(0)-1)
    def _():
        dkv_ref[:heads*HD, :] = dka_ref[...].astype(jnp.bfloat16)
        dkv_ref[heads*HD:, :] = dva_ref[...].astype(jnp.bfloat16)

def attend_back(counts, q_t, g_t, o_t, lse, k, v, bq=256):
    width, rows = q_t.shape
    nk = k.shape[0]
    heads = width//HD
    per = pl.BlockSpec((width,bq), lambda i,c:(0,i))
    whole = pl.BlockSpec((nk,width), lambda i,c:(0,0))
    wide = pl.BlockSpec((2*width,nk), lambda i,c:(0,0))
    return pl.pallas_call(
        functools.partial(attend_back_kernel, heads=heads),
        grid_spec=pltpu.PrefetchScalarGridSpec(
            num_scalar_prefetch=1, grid=(rows//bq,),
            in_specs=[per,per,per,pl.BlockSpec((8,bq), lambda i,c:(0,i)),whole,whole],
            out_specs=[per,wide],
            scratch_shapes=[pltpu.VMEM((width,nk), jnp.bfloat16),pltpu.VMEM((width,nk), jnp.float32),pltpu.VMEM((width,nk), jnp.float32)]),
        out_shape=(jax.ShapeDtypeStruct((width,rows),jnp.bfloat16),)+(jax.ShapeDtypeStruct((2*width,nk),jnp.bfloat16),),
        compiler_params=pltpu.CompilerParams(dimension_semantics=("arbitrary",), vmem_limit_bytes=48<<20),
        name="attend_back",
    )(counts, q_t, g_t, o_t, lse, k, v)


from jax.sharding import Mesh, PartitionSpec as P

D = 768
H = 12
FF = 3072
BLOCK = 256
norm_epsilon = 1e-05
root_half = 0.7071067811865476
density_factor = 0.3989422804014327
DP = ("outer", "mid", "core")
EVERY = ("outer", "mid", "core", "tensor")


def dot_tn(former, latter):
    return lax.dot_general(former, latter, (((0,), (0,)), ((), ())), preferred_element_type=jnp.float32)


def dot_tt(former, latter):
    return lax.dot_general(former, latter, (((0,), (1,)), ((), ())), preferred_element_type=jnp.float32)


def normed_of(summed):
    centered = summed - jnp.mean(summed, axis=-1, keepdims=True)
    inverse = lax.rsqrt(jnp.mean(centered * centered, axis=-1, keepdims=True) + norm_epsilon)
    return centered * inverse, inverse


def layer_norm(summed, norm_gain, norm_shift):
    return normed_of(summed)[0] * norm_gain + norm_shift


def layer_norm_back(upstream, summed, norm_gain):
    normed, inverse = normed_of(summed)
    scaled = upstream * norm_gain
    through = inverse * (
        scaled
        - jnp.mean(scaled, axis=-1, keepdims=True)
        - normed * jnp.mean(scaled * normed, axis=-1, keepdims=True)
    )
    return (through, jnp.sum(upstream * normed, axis=0), jnp.sum(upstream, axis=0))


def units_kernel(x_ref, up_ref, down_ref, bias_ref, active_ref, slope_ref, out_ref, acc_ref):
    i = pl.program_id(0)
    before = dot_nn(x_ref[...], up_ref[0]) + bias_ref[...]
    chance = 0.5 * (1.0 + lax.erf(before * root_half))
    active = (before * chance).astype(jnp.bfloat16)
    active_ref[...] = active
    slope_ref[...] = (chance + before * density_factor * jnp.exp(-0.5 * before * before)).astype(jnp.bfloat16)
    part = dot_nt(active, down_ref[0])

    @pl.when(i == 0)
    def _():
        acc_ref[...] = part

    @pl.when(i > 0)
    def _():
        acc_ref[...] += part

    @pl.when(i == pl.num_programs(0) - 1)
    def _():
        out_ref[...] = acc_ref[...]


def units(x, both, bias):
    rows, width = x.shape
    count = both.shape[0]
    local = both.shape[2] // 2
    cols = pl.BlockSpec((rows, local), lambda i: (0, i))
    return pl.pallas_call(
        units_kernel,
        grid=(count,),
        in_specs=[pl.BlockSpec((rows, width), lambda i: (0, 0)),
                  pl.BlockSpec((1, width, local), lambda i: (i, 0, 0)),
                  pl.BlockSpec((1, width, local), lambda i: (i, 0, 1)),
                  pl.BlockSpec((1, local), lambda i: (0, i))],
        out_specs=[cols, cols, pl.BlockSpec((rows, width), lambda i: (0, 0))],
        scratch_shapes=[pltpu.VMEM((rows, width), jnp.float32)],
        out_shape=(jax.ShapeDtypeStruct((rows, count * local), jnp.bfloat16),) * 2
        + (jax.ShapeDtypeStruct((rows, width), jnp.float32),),
        compiler_params=pltpu.CompilerParams(dimension_semantics=("arbitrary",), vmem_limit_bytes=40 << 20),
        name="units",
    )(x, both, both, bias)


def units_back_kernel(g_ref, up_ref, down_ref, slope_ref, grad_ref, sums_ref, out_ref, acc_ref):
    i = pl.program_id(0)
    grad = (dot_nn(g_ref[...], down_ref[0]) * slope_ref[...].astype(jnp.float32)).astype(jnp.bfloat16)
    grad_ref[...] = grad
    sums_ref[...] = jnp.sum(grad.astype(jnp.float32), axis=0, keepdims=True)
    part = dot_nt(grad, up_ref[0])

    @pl.when(i == 0)
    def _():
        acc_ref[...] = part

    @pl.when(i > 0)
    def _():
        acc_ref[...] += part

    @pl.when(i == pl.num_programs(0) - 1)
    def _():
        out_ref[...] = acc_ref[...]


def units_back(g, both, slope):
    rows, width = g.shape
    count = both.shape[0]
    local = both.shape[2] // 2
    cols = pl.BlockSpec((rows, local), lambda i: (0, i))
    return pl.pallas_call(
        units_back_kernel,
        grid=(count,),
        in_specs=[pl.BlockSpec((rows, width), lambda i: (0, 0)),
                  pl.BlockSpec((1, width, local), lambda i: (i, 0, 0)),
                  pl.BlockSpec((1, width, local), lambda i: (i, 0, 1)),
                  cols],
        out_specs=[cols, pl.BlockSpec((1, local), lambda i: (0, i)), pl.BlockSpec((rows, width), lambda i: (0, 0))],
        scratch_shapes=[pltpu.VMEM((rows, width), jnp.float32)],
        out_shape=(jax.ShapeDtypeStruct((rows, count * local), jnp.bfloat16),
                   jax.ShapeDtypeStruct((1, count * local), jnp.float32),
                   jax.ShapeDtypeStruct((rows, width), jnp.float32)),
        compiler_params=pltpu.CompilerParams(dimension_semantics=("arbitrary",), vmem_limit_bytes=40 << 20),
        name="units_back",
    )(g, both, both, slope)


def swapped(x, axis):
    return lax.ppermute(x, axis, [(0, 1), (1, 0)])


def gather_axis(x, axis):
    if lax.axis_size(axis) != 2:
        return lax.all_gather(x, axis, axis=0)
    other = swapped(x, axis)
    first = lax.axis_index(axis) == 0
    return jnp.stack([jnp.where(first, x, other), jnp.where(first, other, x)])


def gather_over(x, axes):
    for axis in axes:
        x = gather_axis(x, axis)
    return x


def shifted(piece, step):
    count = lax.axis_size("tensor")
    return lax.ppermute(piece, "tensor", [(i, (i + step) % count) for i in range(count)])


def exchange(take, put, start):
    count = lax.axis_size("tensor")
    rank = lax.axis_index("tensor")
    got = [(shifted(take((rank + s) % count), s), (rank - s) % count) for s in range(1, count)]
    out = put(start, take(rank), rank)
    for piece, source in got:
        out = put(out, piece, source)
    return out


def tokens_to_heads(whole):
    count = lax.axis_size("tensor")
    width = whole.shape[0] // count
    own = whole.shape[1]
    return exchange(
        lambda d: lax.dynamic_slice_in_dim(whole, d * width, width, 0),
        lambda out, piece, s: lax.dynamic_update_slice_in_dim(out, piece, s * own, 1),
        jnp.zeros((width, count * own), whole.dtype),
    )


def heads_to_tokens(mine):
    count = lax.axis_size("tensor")
    width = mine.shape[0]
    own = mine.shape[1] // count
    return exchange(
        lambda d: lax.dynamic_slice_in_dim(mine, d * own, own, 1),
        lambda out, piece, s: lax.dynamic_update_slice_in_dim(out, piece, s * width, 0),
        jnp.zeros((count * width, own), mine.dtype),
    )


def gather_tokens(mine):
    count = lax.axis_size("tensor")
    rank = lax.axis_index("tensor")
    own = mine.shape[0]
    out = jnp.zeros((count * own,) + mine.shape[1:], mine.dtype)
    got = [(shifted(mine, s), (rank - s) % count) for s in range(1, count)]
    out = lax.dynamic_update_slice_in_dim(out, mine, rank * own, 0)
    for piece, source in got:
        out = lax.dynamic_update_slice_in_dim(out, piece, source * own, 0)
    return out


def reduce_columns(partial):
    count = lax.axis_size("tensor")
    rank = lax.axis_index("tensor")
    width = partial.shape[1] // count

    def take(d):
        return lax.dynamic_slice_in_dim(partial, d * width, width, 1)

    total = take(rank).astype(jnp.float32)
    for s in range(1, count):
        total = total + shifted(take((rank + s) % count), s).astype(jnp.float32)
    return total


def reduce_rows(partial):
    return lax.psum_scatter(partial, DP, scatter_dimension=0, tiled=True)


def body(
    inputs,
    encoder_out,
    block_ids,
    out_grad,
    in_weight,
    out_weight,
    up_weight,
    down_weight,
    vectors,
    norm_gains,
    up_bias,
):
    low = jnp.bfloat16
    tensor_count = lax.axis_size("tensor")
    tensor_rank = lax.axis_index("tensor")
    width = D // tensor_count
    scale = HD ** (-0.5)
    start = tensor_rank * width
    rows = inputs[0]
    ids = block_ids[0]

    in_low = in_weight.astype(low)
    shards = in_low.shape[1]
    hidden_self = lax.all_gather(rows, "tensor", axis=0, tiled=True)
    head_pack = jnp.concatenate([in_low[0], in_low[1], in_low[2], in_low[4], in_low[5]], axis=1)
    head_pack = gather_over(head_pack, ("core", "mid", "outer")).reshape(D, 5 * width)
    w_self = head_pack[:, : 3 * width]
    w_cross = head_pack[:, 3 * width :]
    out_turned = jnp.swapaxes(out_weight.astype(low), 1, 2)
    mid_pack = jnp.concatenate([in_low[3], out_turned[0], out_turned[1]], axis=1)
    mid_pack = gather_over(gather_tokens(mid_pack).reshape(tensor_count, shards, 3 * width), ("core", "mid", "outer"))
    mid_pack = mid_pack.reshape(D // shards, tensor_count, shards, 3 * width)
    mid_pack = jnp.swapaxes(mid_pack, 0, 1).reshape(tensor_count, D, 3, width)
    turned = jnp.transpose(mid_pack, (2, 0, 3, 1)).reshape(3, D, D)
    wq_cross_t, wo_self, wo_cross = turned[0], turned[1], turned[2]
    unit_pack = jnp.concatenate([up_weight.astype(low), down_weight.astype(low).T], axis=1)
    unit_pack = lax.all_gather(unit_pack, ("tensor",) + DP, axis=0, tiled=True).reshape(tensor_count, D, -1)
    encoder_full = gather_tokens(encoder_out[0])

    head_bias = lax.dynamic_slice_in_dim(vectors[0:4], start, width, 1)
    counts_self = jnp.sum((ids[None, :] <= ids[:, None]).astype(jnp.int32), axis=1)
    counts_cross = jnp.full(ids.shape, encoder_full.shape[0] // KB, jnp.int32)

    q_self = ((dot_tt(w_self[:, :width], hidden_self) + head_bias[0][:, None]) * scale).astype(low)
    k_self = dot_nn(hidden_self, w_self[:, width : 2 * width]).astype(low)
    v_self = (dot_nn(hidden_self, w_self[:, 2 * width :]) + head_bias[1]).astype(low)
    mine_self, lse_self = attend(counts_self, q_self, k_self, v_self)
    k_cross = dot_nn(encoder_full, w_cross[:, :width]).astype(low)
    v_cross = (dot_nn(encoder_full, w_cross[:, width:]) + head_bias[3]).astype(low)
    mixed_self = heads_to_tokens(mine_self)
    summed_one = rows.astype(jnp.float32) + (dot_tn(mixed_self, wo_self) + vectors[4])
    normed_one = layer_norm(summed_one, norm_gains[0], vectors[7])
    hidden_cross = normed_one.astype(low)
    q_cross = tokens_to_heads(((dot_nt(wq_cross_t, hidden_cross) + vectors[2][:, None]) * scale).astype(low))
    mine_cross, lse_cross = attend(counts_cross, q_cross, k_cross, v_cross)
    mixed_cross = heads_to_tokens(mine_cross)
    summed_two = normed_one + (dot_tn(mixed_cross, wo_cross) + vectors[5])
    normed_two = layer_norm(summed_two, norm_gains[1], vectors[8])
    hidden_units = normed_two.astype(low)
    active, slope, unit_out = units(hidden_units, unit_pack, up_bias[None])
    summed_three = normed_two + (unit_out + vectors[6])
    layer_out = layer_norm(summed_three, norm_gains[2], vectors[9]).astype(low)

    grad_three, gain_three, shift_three = layer_norm_back(out_grad[0].astype(jnp.float32), summed_three, norm_gains[2])
    branch_three = grad_three.astype(low)
    bias_down = jnp.sum(branch_three.astype(jnp.float32), axis=0)
    grad_before, unit_bias, unit_back = units_back(branch_three, unit_pack, slope)
    down_grad = reduce_rows(dot_tn(branch_three, active).astype(low))
    up_grad = reduce_rows(dot_tn(hidden_units, grad_before).astype(low))
    grad_two, gain_two, shift_two = layer_norm_back(grad_three + unit_back, summed_two, norm_gains[1])
    branch_two = grad_two.astype(low)
    bias_cross_out = jnp.sum(branch_two.astype(jnp.float32), axis=0)
    grad_mixed_cross = tokens_to_heads(dot_nt(wo_cross, branch_two).astype(low))
    out_grad_cross = reduce_rows(dot_tt(branch_two, mixed_cross).astype(low))
    dq_mine, dkv_cross = attend_back(
        counts_cross, q_cross, grad_mixed_cross, mine_cross, lse_cross, k_cross, v_cross)
    dq_cross = heads_to_tokens(dq_mine)
    kv_grad = reduce_rows(dot_tt(encoder_full, dkv_cross).astype(low))
    encoder_grad = lax.psum_scatter(
        dot_tt(dkv_cross, w_cross).astype(low), "tensor", scatter_dimension=0, tiled=True).astype(jnp.float32)
    bias_query_cross = jnp.sum(dq_cross.astype(jnp.float32), axis=1)
    bias_value_cross = jnp.sum(dkv_cross[width:].astype(jnp.float32), axis=1)
    query_grad_cross = reduce_rows(dot_tt(hidden_cross, dq_cross).astype(low))
    grad_one_in = grad_two + dot_tn(dq_cross, wq_cross_t)
    grad_one, gain_one, shift_one = layer_norm_back(grad_one_in, summed_one, norm_gains[0])
    branch_one = grad_one.astype(low)
    bias_self_out = jnp.sum(branch_one.astype(jnp.float32), axis=0)
    grad_mixed_self = tokens_to_heads(dot_nt(wo_self, branch_one).astype(low))
    out_grad_self = reduce_rows(dot_tt(branch_one, mixed_self).astype(low))
    dq_self, dkv_self = attend_back(
        counts_self, q_self, grad_mixed_self, mine_self, lse_self, k_self, v_self)
    dqkv = jnp.concatenate([dq_self, dkv_self], axis=0)
    input_part = dot_tt(dqkv, w_self).astype(low)
    input_grad = grad_one + lax.psum_scatter(
        input_part, "tensor", scatter_dimension=0, tiled=True).astype(jnp.float32)
    self_grad = reduce_rows(dot_tt(hidden_self, dqkv).astype(low)).astype(jnp.float32)
    bias_query_self = jnp.sum(dq_self.astype(jnp.float32), axis=1)
    bias_value_self = jnp.sum(dkv_self[width:].astype(jnp.float32), axis=1)

    kv_grad = kv_grad.astype(jnp.float32)
    mid_grads = [reduce_columns(g) for g in (query_grad_cross, out_grad_self, out_grad_cross)]
    up_shard = reduce_columns(up_grad)
    down_shard = reduce_columns(down_grad).T
    in_shard = jnp.stack([
        self_grad[:, :width], self_grad[:, width : 2 * width], self_grad[:, 2 * width :],
        mid_grads[0], kv_grad[:, :width], kv_grad[:, width:]])
    out_shard = jnp.stack([mid_grads[1].T, mid_grads[2].T])

    def embed(part):
        return lax.dynamic_update_slice_in_dim(jnp.zeros((D,), jnp.float32), part, start, 0)

    vector_grad = jnp.stack([
        embed(bias_query_self), embed(bias_value_self), bias_query_cross, embed(bias_value_cross),
        bias_self_out, bias_cross_out, bias_down, shift_one, shift_two, shift_three])
    gain_grad = jnp.stack([gain_one, gain_two, gain_three])
    vector_total, gain_total, unit_total = lax.psum((vector_grad, gain_grad, unit_bias[0]), EVERY)
    return (
        layer_out[None],
        input_grad[None],
        encoder_grad[None],
        in_shard,
        out_shard,
        up_shard,
        down_shard,
        vector_total,
        gain_total,
        unit_total,
    )


def solution(mesh):
    devices = mesh.devices
    wide = Mesh(devices.reshape(devices.shape[0] // 4, 2, 2, devices.shape[1]), EVERY)
    return jax.shard_map(
        body,
        mesh=wide,
        in_specs=(
            P(DP, "tensor", None),
            P(DP, "tensor", None),
            P(DP, None),
            P(DP, "tensor", None),
            P(None, DP, "tensor"),
            P(None, "tensor", DP),
            P(DP, "tensor"),
            P("tensor", DP),
            P(),
            P(),
            P(),
        ),
        out_specs=(
            P(DP, "tensor", None),
            P(DP, "tensor", None),
            P(DP, "tensor", None),
            P(None, DP, "tensor"),
            P(None, "tensor", DP),
            P(DP, "tensor"),
            P("tensor", DP),
            P(),
            P(),
            P(),
        ),
        check_vma=False,
    )
```

```python
import functools
import jax, jax.numpy as jnp
from jax import lax
from jax.experimental import pallas as pl
from jax.experimental.pallas import tpu as pltpu
HD=64
KB=256
def dot_nn(a,b): return jnp.dot(a,b,preferred_element_type=jnp.float32)
def dot_nt(a,b): return lax.dot_general(a,b,(((1,),(1,)),((),())),preferred_element_type=jnp.float32)

def over_chunks(count, blocks, step, carry):
    done = 0
    while True:
        def chunk(j, carry, blocks=blocks, done=done):
            return step(pl.multiple_of((done + j * blocks) * KB, KB), blocks * KB, carry)
        trips = (count - done) // blocks
        carry = lax.fori_loop(0, trips, chunk, carry)
        if blocks == 1:
            return carry
        done = done + trips * blocks
        blocks //= 2

def head_masked(block, h):
    rows = lax.broadcasted_iota(jnp.int32, block.shape, 0)
    return jnp.where((rows >= h*HD) & (rows < (h+1)*HD), block, jnp.zeros_like(block))

def attend_kernel(counts_ref, q_ref, k_ref, v_ref, o_ref, lse_ref, vt_ref, *, heads, blocks):
    i = pl.program_id(0)
    nk = k_ref.shape[0]//KB
    bq = q_ref.shape[1]
    @pl.when(i == 0)
    def _():
        for j in range(nk):
            vt_ref[:, j*KB:(j+1)*KB] = v_ref[j*KB:(j+1)*KB, :].T
    q = q_ref[...]
    qm = [head_masked(q, h) for h in range(heads)]
    def step(start, keys, carry):
        kj = k_ref[pl.ds(start, keys), :]
        new = []
        for h in range(heads):
            m, l, acc = carry[h]
            s = dot_nn(kj, qm[h])
            m_new = jnp.maximum(m, jnp.max(s, axis=0, keepdims=True))
            p = jnp.exp(s - m_new)
            alpha = jnp.exp(m - m_new)
            l = l*alpha + jnp.sum(p, axis=0, keepdims=True)
            vt = vt_ref[h*HD:(h+1)*HD, pl.ds(start, keys)]
            acc = acc*alpha + dot_nn(vt, p.astype(jnp.bfloat16))
            new.append((m_new, l, acc))
        return tuple(new)
    init = tuple((jnp.full((1,bq),-1e30,jnp.float32), jnp.zeros((1,bq),jnp.float32), jnp.zeros((HD,bq),jnp.float32)) for _ in range(heads))
    fin = over_chunks(counts_ref[i], blocks, step, init)
    for h in range(heads):
        m, l, acc = fin[h]
        o_ref[h*HD:(h+1)*HD, :] = (acc/l).astype(jnp.bfloat16)
        lse_ref[h:h+1, :] = m + jnp.log(l)

def attend(counts, q_t, k, v, bq=256, blocks=4):
    width, rows = q_t.shape
    nk = k.shape[0]
    heads = width//HD
    return pl.pallas_call(
        functools.partial(attend_kernel, heads=heads, blocks=blocks),
        grid_spec=pltpu.PrefetchScalarGridSpec(
            num_scalar_prefetch=1, grid=(rows//bq,),
            in_specs=[pl.BlockSpec((width,bq), lambda i,c:(0,i)),
                      pl.BlockSpec((nk,width), lambda i,c:(0,0)),
                      pl.BlockSpec((nk,width), lambda i,c:(0,0))],
            out_specs=[pl.BlockSpec((width,bq), lambda i,c:(0,i)),
                       pl.BlockSpec((8,bq), lambda i,c:(0,i))],
            scratch_shapes=[pltpu.VMEM((width,nk), jnp.bfloat16)]),
        out_shape=(jax.ShapeDtypeStruct((width,rows),jnp.bfloat16), jax.ShapeDtypeStruct((8,rows),jnp.float32)),
        compiler_params=pltpu.CompilerParams(dimension_semantics=("arbitrary",), vmem_limit_bytes=40<<20),
        cost_estimate=pl.CostEstimate(flops=4*rows*nk*width*4, transcendentals=rows*nk*heads, bytes_accessed=8*rows*width),
        name="attend",
    )(counts, q_t, k, v)

def attend_back_kernel(counts_ref, q_ref, g_ref, o_ref, lse_ref, k_ref, v_ref, dq_ref, dkv_ref, kt_ref, dka_ref, dva_ref, *, heads, blocks):
    i = pl.program_id(0)
    nk = k_ref.shape[0]//KB
    bq = q_ref.shape[1]
    @pl.when(i == 0)
    def _():
        for j in range(nk):
            kt_ref[:, j*KB:(j+1)*KB] = k_ref[j*KB:(j+1)*KB, :].T
        dka_ref[...] = jnp.zeros_like(dka_ref)
        dva_ref[...] = jnp.zeros_like(dva_ref)
    q = q_ref[...]
    g = g_ref[...]
    prod = g.astype(jnp.float32)*o_ref[...].astype(jnp.float32)
    qm = [head_masked(q, h) for h in range(heads)]
    gm = [head_masked(g, h) for h in range(heads)]
    delta = [jnp.sum(prod[h*HD:(h+1)*HD], axis=0, keepdims=True) for h in range(heads)]
    lse = [lse_ref[h:h+1, :] for h in range(heads)]
    def step(start, keys, carry):
        kj = k_ref[pl.ds(start, keys), :]
        vj = v_ref[pl.ds(start, keys), :]
        new = []
        for h in range(heads):
            lo, hi = h*HD, (h+1)*HD
            p = jnp.exp(dot_nn(kj, qm[h]) - lse[h])
            dp = dot_nn(vj, gm[h])
            ds = (p*(dp - delta[h])).astype(jnp.bfloat16)
            dva_ref[lo:hi, pl.ds(start, keys)] += dot_nt(g[lo:hi], p.astype(jnp.bfloat16))
            dka_ref[lo:hi, pl.ds(start, keys)] += dot_nt(q[lo:hi], ds)
            new.append(carry[h] + dot_nn(kt_ref[lo:hi, pl.ds(start, keys)], ds))
        return tuple(new)
    fin = over_chunks(counts_ref[i], blocks, step, tuple(jnp.zeros((HD,bq),jnp.float32) for _ in range(heads)))
    for h in range(heads):
        dq_ref[h*HD:(h+1)*HD, :] = (fin[h] * HD**-0.5).astype(jnp.bfloat16)
    @pl.when(i == pl.num_programs(0)-1)
    def _():
        dkv_ref[:heads*HD, :] = dka_ref[...].astype(jnp.bfloat16)
        dkv_ref[heads*HD:, :] = dva_ref[...].astype(jnp.bfloat16)

def attend_back(counts, q_t, g_t, o_t, lse, k, v, bq=256, blocks=4):
    width, rows = q_t.shape
    nk = k.shape[0]
    heads = width//HD
    per = pl.BlockSpec((width,bq), lambda i,c:(0,i))
    whole = pl.BlockSpec((nk,width), lambda i,c:(0,0))
    wide = pl.BlockSpec((2*width,nk), lambda i,c:(0,0))
    return pl.pallas_call(
        functools.partial(attend_back_kernel, heads=heads, blocks=blocks),
        grid_spec=pltpu.PrefetchScalarGridSpec(
            num_scalar_prefetch=1, grid=(rows//bq,),
            in_specs=[per,per,per,pl.BlockSpec((8,bq), lambda i,c:(0,i)),whole,whole],
            out_specs=[per,wide],
            scratch_shapes=[pltpu.VMEM((width,nk), jnp.bfloat16),pltpu.VMEM((width,nk), jnp.float32),pltpu.VMEM((width,nk), jnp.float32)]),
        out_shape=(jax.ShapeDtypeStruct((width,rows),jnp.bfloat16),)+(jax.ShapeDtypeStruct((2*width,nk),jnp.bfloat16),),
        compiler_params=pltpu.CompilerParams(dimension_semantics=("arbitrary",), vmem_limit_bytes=48<<20),
        cost_estimate=pl.CostEstimate(flops=10*rows*nk*width*4, transcendentals=rows*nk*heads, bytes_accessed=16*rows*width),
        name="attend_back",
    )(counts, q_t, g_t, o_t, lse, k, v)


from jax.sharding import Mesh, PartitionSpec as P

D = 768
H = 12
FF = 3072
BLOCK = 256
norm_epsilon = 1e-05
root_half = 0.7071067811865476
density_factor = 0.3989422804014327
DP = ("outer", "mid", "core")
EVERY = ("outer", "mid", "core", "tensor")


def dot_tn(former, latter):
    return lax.dot_general(former, latter, (((0,), (0,)), ((), ())), preferred_element_type=jnp.float32)


def dot_tt(former, latter):
    return lax.dot_general(former, latter, (((0,), (1,)), ((), ())), preferred_element_type=jnp.float32)


def normed_of(summed):
    centered = summed - jnp.mean(summed, axis=-1, keepdims=True)
    inverse = lax.rsqrt(jnp.mean(centered * centered, axis=-1, keepdims=True) + norm_epsilon)
    return centered * inverse, inverse


def layer_norm(summed, norm_gain, norm_shift):
    return normed_of(summed)[0] * norm_gain + norm_shift


def layer_norm_back(upstream, summed, norm_gain):
    normed, inverse = normed_of(summed)
    scaled = upstream * norm_gain
    through = inverse * (
        scaled
        - jnp.mean(scaled, axis=-1, keepdims=True)
        - normed * jnp.mean(scaled * normed, axis=-1, keepdims=True)
    )
    return (through, jnp.sum(upstream * normed, axis=0), jnp.sum(upstream, axis=0))


def units_kernel(x_ref, up_ref, down_ref, bias_ref, active_ref, slope_ref, out_ref, acc_ref):
    i = pl.program_id(0)
    before = dot_nn(x_ref[...], up_ref[0]) + bias_ref[...]
    chance = 0.5 * (1.0 + lax.erf(before * root_half))
    active = (before * chance).astype(jnp.bfloat16)
    active_ref[...] = active
    slope_ref[...] = (chance + before * density_factor * jnp.exp(-0.5 * before * before)).astype(jnp.bfloat16)
    part = dot_nt(active, down_ref[0])

    @pl.when(i == 0)
    def _():
        acc_ref[...] = part

    @pl.when(i > 0)
    def _():
        acc_ref[...] += part

    @pl.when(i == pl.num_programs(0) - 1)
    def _():
        out_ref[...] = acc_ref[...]


def units(x, both, bias):
    rows, width = x.shape
    count = both.shape[0]
    local = both.shape[2] // 2
    cols = pl.BlockSpec((rows, local), lambda i: (0, i))
    return pl.pallas_call(
        units_kernel,
        grid=(count,),
        in_specs=[pl.BlockSpec((rows, width), lambda i: (0, 0)),
                  pl.BlockSpec((1, width, local), lambda i: (i, 0, 0)),
                  pl.BlockSpec((1, width, local), lambda i: (i, 0, 1)),
                  pl.BlockSpec((1, local), lambda i: (0, i))],
        out_specs=[cols, cols, pl.BlockSpec((rows, width), lambda i: (0, 0))],
        scratch_shapes=[pltpu.VMEM((rows, width), jnp.float32)],
        out_shape=(jax.ShapeDtypeStruct((rows, count * local), jnp.bfloat16),) * 2
        + (jax.ShapeDtypeStruct((rows, width), jnp.float32),),
        compiler_params=pltpu.CompilerParams(dimension_semantics=("arbitrary",), vmem_limit_bytes=40 << 20),
        name="units",
    )(x, both, both, bias)


def units_back_kernel(g_ref, up_ref, down_ref, slope_ref, grad_ref, sums_ref, out_ref, acc_ref):
    i = pl.program_id(0)
    grad = (dot_nn(g_ref[...], down_ref[0]) * slope_ref[...].astype(jnp.float32)).astype(jnp.bfloat16)
    grad_ref[...] = grad
    sums_ref[...] = jnp.sum(grad.astype(jnp.float32), axis=0, keepdims=True)
    part = dot_nt(grad, up_ref[0])

    @pl.when(i == 0)
    def _():
        acc_ref[...] = part

    @pl.when(i > 0)
    def _():
        acc_ref[...] += part

    @pl.when(i == pl.num_programs(0) - 1)
    def _():
        out_ref[...] = acc_ref[...]


def units_back(g, both, slope):
    rows, width = g.shape
    count = both.shape[0]
    local = both.shape[2] // 2
    cols = pl.BlockSpec((rows, local), lambda i: (0, i))
    return pl.pallas_call(
        units_back_kernel,
        grid=(count,),
        in_specs=[pl.BlockSpec((rows, width), lambda i: (0, 0)),
                  pl.BlockSpec((1, width, local), lambda i: (i, 0, 0)),
                  pl.BlockSpec((1, width, local), lambda i: (i, 0, 1)),
                  cols],
        out_specs=[cols, pl.BlockSpec((1, local), lambda i: (0, i)), pl.BlockSpec((rows, width), lambda i: (0, 0))],
        scratch_shapes=[pltpu.VMEM((rows, width), jnp.float32)],
        out_shape=(jax.ShapeDtypeStruct((rows, count * local), jnp.bfloat16),
                   jax.ShapeDtypeStruct((1, count * local), jnp.float32),
                   jax.ShapeDtypeStruct((rows, width), jnp.float32)),
        compiler_params=pltpu.CompilerParams(dimension_semantics=("arbitrary",), vmem_limit_bytes=40 << 20),
        name="units_back",
    )(g, both, both, slope)


def swapped(x, axis):
    return lax.ppermute(x, axis, [(0, 1), (1, 0)])


def gather_axis(x, axis):
    if lax.axis_size(axis) != 2:
        return lax.all_gather(x, axis, axis=0)
    other = swapped(x, axis)
    place = lax.broadcasted_iota(jnp.int32, (2,) + (1,) * x.ndim, 0)
    return jnp.where(place == lax.axis_index(axis), x[None], other[None])


def gather_over(x, axes):
    for axis in axes:
        x = gather_axis(x, axis)
    return x


def shifted(piece, step):
    count = lax.axis_size("tensor")
    return lax.ppermute(piece, "tensor", [(i, (i + step) % count) for i in range(count)])


def exchange(take, put, start):
    count = lax.axis_size("tensor")
    rank = lax.axis_index("tensor")
    got = [(shifted(take((rank + s) % count), s), (rank - s) % count) for s in range(1, count)]
    out = put(start, take(rank), rank)
    for piece, source in got:
        out = put(out, piece, source)
    return out


def tokens_to_heads(whole):
    count = lax.axis_size("tensor")
    width = whole.shape[0] // count
    own = whole.shape[1]
    return exchange(
        lambda d: lax.dynamic_slice_in_dim(whole, d * width, width, 0),
        lambda out, piece, s: lax.dynamic_update_slice_in_dim(out, piece, s * own, 1),
        jnp.zeros((width, count * own), whole.dtype),
    )


def heads_to_tokens(mine):
    count = lax.axis_size("tensor")
    width = mine.shape[0]
    own = mine.shape[1] // count
    return exchange(
        lambda d: lax.dynamic_slice_in_dim(mine, d * own, own, 1),
        lambda out, piece, s: lax.dynamic_update_slice_in_dim(out, piece, s * width, 0),
        jnp.zeros((count * width, own), mine.dtype),
    )


def gather_tokens(mine):
    count = lax.axis_size("tensor")
    rank = lax.axis_index("tensor")
    own = mine.shape[0]
    out = jnp.zeros((count * own,) + mine.shape[1:], mine.dtype)
    got = [(shifted(mine, s), (rank - s) % count) for s in range(1, count)]
    out = lax.dynamic_update_slice_in_dim(out, mine, rank * own, 0)
    for piece, source in got:
        out = lax.dynamic_update_slice_in_dim(out, piece, source * own, 0)
    return out


def reduce_columns(partial):
    count = lax.axis_size("tensor")
    rank = lax.axis_index("tensor")
    width = partial.shape[1] // count

    def take(d):
        return lax.dynamic_slice_in_dim(partial, d * width, width, 1)

    total = take(rank).astype(jnp.float32)
    for s in range(1, count):
        total = total + shifted(take((rank + s) % count), s).astype(jnp.float32)
    return total


def tied(*values):
    return lax.optimization_barrier(values)


def parted(x, axis, dim):
    rank = lax.axis_index(axis)
    return (lax.dynamic_index_in_dim(x, rank, dim, keepdims=False),
            lax.dynamic_index_in_dim(x, 1 - rank, dim, keepdims=False))


class Flow:
    def __init__(self, former, latter, axes):
        self.axes = axes
        self.pairs = all(lax.axis_size(a) == 2 for a in DP)
        if not self.pairs:
            self.moving = reduce_rows(dot_tn(former, latter).astype(jnp.bfloat16))
            return
        rows = former.shape[1] // lax.axis_size(DP)
        mine, theirs = parted(former.reshape(-1, lax.axis_size(DP) // 2, 2, rows), "core", 2)
        self.kept = dot_tn(mine.reshape(former.shape[0], -1), latter).astype(jnp.bfloat16)
        self.sent = dot_tn(theirs.reshape(former.shape[0], -1), latter).astype(jnp.bfloat16)

    @classmethod
    def of(cls, partial, axes):
        self = cls.__new__(cls)
        self.axes = axes
        self.pairs = all(lax.axis_size(a) == 2 for a in DP)
        if not self.pairs:
            self.moving = reduce_rows(partial)
            return self
        count = lax.axis_size(DP)
        rows, cols = partial.shape[0] // count, partial.shape[1]
        mine, theirs = parted(partial.reshape(count // 2, 2, rows, cols), "core", 1)
        self.kept, self.sent = mine.reshape(-1, cols), theirs.reshape(-1, cols)
        return self

    def across_core(self):
        if self.pairs:
            self.moving = swapped(self.sent, "core")

    def across(self, stage):
        if not self.pairs:
            return
        if stage == 0:
            whole = (2, 2, -1) + self.kept.shape[1:]
            kept, got = self.kept.reshape(whole), self.moving.reshape(whole)
            dim = DP.index(self.axes[0])
        else:
            kept, got, dim = self.kept, self.moving, 0
        pieces = zip(parted(kept, self.axes[stage], dim), parted(got, self.axes[stage], dim))
        keep, send = [(a.astype(jnp.float32) + b.astype(jnp.float32)).astype(jnp.bfloat16) for a, b in pieces]
        self.kept, self.moving = keep, swapped(send, self.axes[stage])

    def total(self):
        if not self.pairs:
            return self.moving
        return (self.kept.astype(jnp.float32) + self.moving.astype(jnp.float32)).astype(jnp.bfloat16)


def reduce_rows(partial):
    return lax.psum_scatter(partial, DP, scatter_dimension=0, tiled=True)


def body(
    inputs,
    encoder_out,
    block_ids,
    out_grad,
    in_weight,
    out_weight,
    up_weight,
    down_weight,
    vectors,
    norm_gains,
    up_bias,
):
    low = jnp.bfloat16
    tensor_count = lax.axis_size("tensor")
    tensor_rank = lax.axis_index("tensor")
    width = D // tensor_count
    scale = HD ** (-0.5)
    start = tensor_rank * width
    rows = inputs[0]
    ids = block_ids[0]

    in_low = in_weight.astype(low)
    shards = in_low.shape[1]
    hidden_self = lax.all_gather(rows, "tensor", axis=0, tiled=True)
    head_pack = jnp.concatenate([in_low[0], in_low[1], in_low[2], in_low[4], in_low[5]], axis=1)
    head_pack = gather_over(head_pack, ("core", "mid", "outer")).reshape(D, 5 * width)
    w_self = head_pack[:, : 3 * width]
    w_cross = head_pack[:, 3 * width :]
    out_turned = jnp.swapaxes(out_weight.astype(low), 1, 2)
    mid_pack = jnp.concatenate([in_low[3], out_turned[0], out_turned[1]], axis=1)
    encoder, mid_pack, hidden_self = tied(encoder_out[0], mid_pack, hidden_self)
    mid_pack = gather_over(gather_tokens(mid_pack).reshape(tensor_count, shards, 3 * width), ("core", "mid", "outer"))
    mid_pack = mid_pack.reshape(D // shards, tensor_count, shards, 3, width)
    wq_cross, wo_self, wo_cross = (
        jnp.swapaxes(mid_pack[:, :, :, n], 1, 2).reshape(D, D) for n in range(3))
    unit_pack = jnp.concatenate([up_weight.astype(low), down_weight.astype(low).T], axis=1)
    unit_pack = lax.all_gather(unit_pack, ("tensor",) + DP, axis=0, tiled=True).reshape(tensor_count, D, -1)
    encoder_full = gather_tokens(encoder)

    head_bias = lax.dynamic_slice_in_dim(vectors[0:4], start, width, 1)
    counts_self = jnp.sum((ids[None, :] <= ids[:, None]).astype(jnp.int32), axis=1)
    counts_cross = jnp.full((ids.shape[0] // 2,), encoder_full.shape[0] // KB, jnp.int32)

    q_self = ((dot_tt(w_self[:, :width], hidden_self) + head_bias[0][:, None]) * scale).astype(low)
    k_self = dot_nn(hidden_self, w_self[:, width : 2 * width]).astype(low)
    v_self = (dot_nn(hidden_self, w_self[:, 2 * width :]) + head_bias[1]).astype(low)
    mine_self, lse_self = attend(counts_self, q_self, k_self, v_self)
    k_cross = dot_nn(encoder_full, w_cross[:, :width]).astype(low)
    v_cross = (dot_nn(encoder_full, w_cross[:, width:]) + head_bias[3]).astype(low)
    mixed_self = heads_to_tokens(mine_self)
    summed_one = rows.astype(jnp.float32) + (dot_tt(mixed_self, wo_self) + vectors[4])
    normed_one = layer_norm(summed_one, norm_gains[0], vectors[7])
    hidden_cross = normed_one.astype(low)
    q_cross = tokens_to_heads(((dot_tt(wq_cross, hidden_cross) + vectors[2][:, None]) * scale).astype(low))
    mine_cross, lse_cross = attend(counts_cross, q_cross, k_cross, v_cross, bq=512)
    mixed_cross = heads_to_tokens(mine_cross)
    summed_two = normed_one + (dot_tt(mixed_cross, wo_cross) + vectors[5])
    normed_two = layer_norm(summed_two, norm_gains[1], vectors[8])
    hidden_units = normed_two.astype(low)
    active, slope, unit_out = units(hidden_units, unit_pack, up_bias[None])
    summed_three = normed_two + (unit_out + vectors[6])
    layer_out = layer_norm(summed_three, norm_gains[2], vectors[9]).astype(low)

    grad_three, gain_three, shift_three = layer_norm_back(out_grad[0].astype(jnp.float32), summed_three, norm_gains[2])
    branch_three = grad_three.astype(low)
    bias_down = jnp.sum(branch_three.astype(jnp.float32), axis=0)
    grad_before, unit_bias, unit_back = units_back(branch_three, unit_pack, slope)
    grad_two, gain_two, shift_two = layer_norm_back(grad_three + unit_back, summed_two, norm_gains[1])
    branch_two = grad_two.astype(low)
    bias_cross_out = jnp.sum(branch_two.astype(jnp.float32), axis=0)
    down = Flow(branch_three, active, ("mid", "outer"))
    up = Flow(hidden_units, grad_before, ("outer", "mid"))
    grad_mixed_cross = tokens_to_heads(dot_tt(wo_cross, branch_two).astype(low))
    out_grad_cross = dot_tt(branch_two, mixed_cross).astype(low)
    if down.pairs:
        grad_mixed_cross, out_grad_cross, down.kept, down.sent, up.kept, up.sent = tied(
            grad_mixed_cross, out_grad_cross, down.kept, down.sent, up.kept, up.sent)
    down.across_core()
    up.across_core()
    dq_mine, dkv_cross = attend_back(
        counts_cross, q_cross, grad_mixed_cross, mine_cross, lse_cross, k_cross, v_cross, bq=512)
    dq_mine, dkv_cross, down.moving, up.moving = tied(dq_mine, dkv_cross, down.moving, up.moving)
    encoder_part = lax.psum_scatter(
        dot_tt(dkv_cross, w_cross).astype(low), "tensor", scatter_dimension=0, tiled=True)
    kv_grad = dot_tt(encoder_full, dkv_cross).astype(low)
    dq_cross = heads_to_tokens(dq_mine)
    bias_query_cross = jnp.sum(dq_cross.astype(jnp.float32), axis=1)
    bias_value_cross = jnp.sum(dkv_cross[width:].astype(jnp.float32), axis=1)
    down.across(0)
    up.across(0)
    query_grad_cross = dot_tt(hidden_cross, dq_cross).astype(low)
    cross_grads = reduce_rows(jnp.concatenate([query_grad_cross, out_grad_cross, kv_grad], axis=1))
    grad_one_in = grad_two + dot_tt(dq_cross, wq_cross)
    grad_one, gain_one, shift_one = layer_norm_back(grad_one_in, summed_one, norm_gains[0])
    branch_one = grad_one.astype(low)
    bias_self_out = jnp.sum(branch_one.astype(jnp.float32), axis=0)
    grad_mixed_self = tokens_to_heads(dot_tt(wo_self, branch_one).astype(low))
    out_grad_self = dot_tt(branch_one, mixed_self).astype(low)
    grad_mixed_self, down.moving, up.moving, out_grad_self, encoder_part = tied(
        grad_mixed_self, down.moving, up.moving, out_grad_self, encoder_part)
    down.across(1)
    up.across(1)
    dq_self, dkv_self = attend_back(
        counts_self, q_self, grad_mixed_self, mine_self, lse_self, k_self, v_self)
    dq_self, dkv_self, down.moving, up.moving, cross_grads = tied(
        dq_self, dkv_self, down.moving, up.moving, cross_grads)
    dqkv = jnp.concatenate([dq_self, dkv_self], axis=0)
    input_part = dot_tt(dqkv, w_self).astype(low)
    input_part, dqkv = tied(input_part, dqkv)
    input_grad = grad_one + lax.psum_scatter(
        input_part, "tensor", scatter_dimension=0, tiled=True).astype(jnp.float32)
    self_flow = Flow.of(
        jnp.concatenate([out_grad_self, dot_tt(hidden_self, dqkv).astype(low)], axis=1), ("mid", "outer"))
    self_flow.across_core()
    self_flow.across(0)
    self_flow.across(1)
    self_grads = self_flow.total()
    bias_query_self = jnp.sum(dq_self.astype(jnp.float32), axis=1)
    bias_value_self = jnp.sum(dkv_self[width:].astype(jnp.float32), axis=1)

    encoder_grad = encoder_part.astype(jnp.float32)
    query_shard = reduce_columns(cross_grads[:, :D])
    out_shard = jnp.stack([reduce_columns(self_grads[:, :D]).T, reduce_columns(cross_grads[:, D : 2 * D]).T])
    kv_shard = cross_grads[:, 2 * D :].astype(jnp.float32)
    self_shard = self_grads[:, D:].astype(jnp.float32)
    up_shard = reduce_columns(up.total())
    down_shard = reduce_columns(down.total()).T
    in_shard = jnp.stack([
        self_shard[:, :width], self_shard[:, width : 2 * width], self_shard[:, 2 * width :],
        query_shard, kv_shard[:, :width], kv_shard[:, width:]])

    def embed(part):
        return lax.dynamic_update_slice_in_dim(jnp.zeros((D,), jnp.float32), part, start, 0)

    vector_grad = jnp.stack([
        embed(bias_query_self), embed(bias_value_self), bias_query_cross, embed(bias_value_cross),
        bias_self_out, bias_cross_out, bias_down, shift_one, shift_two, shift_three])
    gain_grad = jnp.stack([gain_one, gain_two, gain_three])
    vector_total, gain_total, unit_total = lax.psum((vector_grad, gain_grad, unit_bias[0]), EVERY)
    return (
        layer_out[None],
        input_grad[None],
        encoder_grad[None],
        in_shard,
        out_shard,
        up_shard,
        down_shard,
        vector_total,
        gain_total,
        unit_total,
    )


def solution(mesh):
    devices = mesh.devices
    wide = Mesh(devices.reshape(devices.shape[0] // 4, 2, 2, devices.shape[1]), EVERY)
    return jax.shard_map(
        body,
        mesh=wide,
        in_specs=(
            P(DP, "tensor", None),
            P(DP, "tensor", None),
            P(DP, None),
            P(DP, "tensor", None),
            P(None, DP, "tensor"),
            P(None, "tensor", DP),
            P(DP, "tensor"),
            P("tensor", DP),
            P(),
            P(),
            P(),
        ),
        out_specs=(
            P(DP, "tensor", None),
            P(DP, "tensor", None),
            P(DP, "tensor", None),
            P(None, DP, "tensor"),
            P(None, "tensor", DP),
            P(DP, "tensor"),
            P("tensor", DP),
            P(),
            P(),
            P(),
        ),
        check_vma=False,
    )
```

```python
import functools
import jax, jax.numpy as jnp
from jax import lax
from jax.experimental import pallas as pl
from jax.experimental.pallas import tpu as pltpu
HD=64
KB=256
def dot_nn(a,b): return jnp.dot(a,b,preferred_element_type=jnp.float32)
def dot_nt(a,b): return lax.dot_general(a,b,(((1,),(1,)),((),())),preferred_element_type=jnp.float32)

def over_chunks(count, blocks, step, carry):
    done = 0
    while True:
        def chunk(j, carry, blocks=blocks, done=done):
            return step(pl.multiple_of((done + j * blocks) * KB, KB), blocks * KB, carry)
        trips = (count - done) // blocks
        carry = lax.fori_loop(0, trips, chunk, carry)
        if blocks == 1:
            return carry
        done = done + trips * blocks
        blocks //= 2

def head_masked(block, h):
    rows = lax.broadcasted_iota(jnp.int32, block.shape, 0)
    return jnp.where((rows >= h*HD) & (rows < (h+1)*HD), block, jnp.zeros_like(block))

def attend_kernel(counts_ref, q_ref, k_ref, v_ref, o_ref, lse_ref, vt_ref, *, heads, blocks):
    i = pl.program_id(0)
    nk = k_ref.shape[0]//KB
    bq = q_ref.shape[1]
    @pl.when(i == 0)
    def _():
        for j in range(nk):
            vt_ref[:, j*KB:(j+1)*KB] = v_ref[j*KB:(j+1)*KB, :].T
    q = q_ref[...]
    qm = [head_masked(q, h) for h in range(heads)]
    def step(start, keys, carry):
        kj = k_ref[pl.ds(start, keys), :]
        new = []
        for h in range(heads):
            m, l, acc = carry[h]
            s = dot_nn(kj, qm[h])
            m_new = jnp.maximum(m, jnp.max(s, axis=0, keepdims=True))
            p = jnp.exp(s - m_new)
            alpha = jnp.exp(m - m_new)
            l = l*alpha + jnp.sum(p, axis=0, keepdims=True)
            vt = vt_ref[h*HD:(h+1)*HD, pl.ds(start, keys)]
            acc = acc*alpha + dot_nn(vt, p.astype(jnp.bfloat16))
            new.append((m_new, l, acc))
        return tuple(new)
    init = tuple((jnp.full((1,bq),-1e30,jnp.float32), jnp.zeros((1,bq),jnp.float32), jnp.zeros((HD,bq),jnp.float32)) for _ in range(heads))
    fin = over_chunks(counts_ref[i], blocks, step, init)
    for h in range(heads):
        m, l, acc = fin[h]
        o_ref[h*HD:(h+1)*HD, :] = (acc/l).astype(jnp.bfloat16)
        lse_ref[h:h+1, :] = m + jnp.log(l)

def attend(counts, q_t, k, v, bq=256, blocks=4):
    width, rows = q_t.shape
    nk = k.shape[0]
    heads = width//HD
    return pl.pallas_call(
        functools.partial(attend_kernel, heads=heads, blocks=blocks),
        grid_spec=pltpu.PrefetchScalarGridSpec(
            num_scalar_prefetch=1, grid=(rows//bq,),
            in_specs=[pl.BlockSpec((width,bq), lambda i,c:(0,i)),
                      pl.BlockSpec((nk,width), lambda i,c:(0,0)),
                      pl.BlockSpec((nk,width), lambda i,c:(0,0))],
            out_specs=[pl.BlockSpec((width,bq), lambda i,c:(0,i)),
                       pl.BlockSpec((8,bq), lambda i,c:(0,i))],
            scratch_shapes=[pltpu.VMEM((width,nk), jnp.bfloat16)]),
        out_shape=(jax.ShapeDtypeStruct((width,rows),jnp.bfloat16), jax.ShapeDtypeStruct((8,rows),jnp.float32)),
        compiler_params=pltpu.CompilerParams(dimension_semantics=("arbitrary",), vmem_limit_bytes=40<<20),
        cost_estimate=pl.CostEstimate(flops=4*rows*nk*width*4, transcendentals=rows*nk*heads, bytes_accessed=8*rows*width),
        name="attend",
    )(counts, q_t, k, v)

def attend_back_kernel(counts_ref, q_ref, g_ref, o_ref, lse_ref, k_ref, v_ref, dq_ref, dkv_ref, kt_ref, dka_ref, dva_ref, *, heads, blocks):
    i = pl.program_id(0)
    nk = k_ref.shape[0]//KB
    bq = q_ref.shape[1]
    @pl.when(i == 0)
    def _():
        for j in range(nk):
            kt_ref[:, j*KB:(j+1)*KB] = k_ref[j*KB:(j+1)*KB, :].T
        dka_ref[...] = jnp.zeros_like(dka_ref)
        dva_ref[...] = jnp.zeros_like(dva_ref)
    q = q_ref[...]
    g = g_ref[...]
    prod = g.astype(jnp.float32)*o_ref[...].astype(jnp.float32)
    qm = [head_masked(q, h) for h in range(heads)]
    gm = [head_masked(g, h) for h in range(heads)]
    delta = [jnp.sum(prod[h*HD:(h+1)*HD], axis=0, keepdims=True) for h in range(heads)]
    lse = [lse_ref[h:h+1, :] for h in range(heads)]
    def step(start, keys, carry):
        kj = k_ref[pl.ds(start, keys), :]
        vj = v_ref[pl.ds(start, keys), :]
        new = []
        for h in range(heads):
            lo, hi = h*HD, (h+1)*HD
            p = jnp.exp(dot_nn(kj, qm[h]) - lse[h])
            dp = dot_nn(vj, gm[h])
            ds = (p*(dp - delta[h])).astype(jnp.bfloat16)
            dva_ref[lo:hi, pl.ds(start, keys)] += dot_nt(g[lo:hi], p.astype(jnp.bfloat16))
            dka_ref[lo:hi, pl.ds(start, keys)] += dot_nt(q[lo:hi], ds)
            new.append(carry[h] + dot_nn(kt_ref[lo:hi, pl.ds(start, keys)], ds))
        return tuple(new)
    fin = over_chunks(counts_ref[i], blocks, step, tuple(jnp.zeros((HD,bq),jnp.float32) for _ in range(heads)))
    for h in range(heads):
        dq_ref[h*HD:(h+1)*HD, :] = (fin[h] * HD**-0.5).astype(jnp.bfloat16)
    @pl.when(i == pl.num_programs(0)-1)
    def _():
        dkv_ref[:heads*HD, :] = dka_ref[...].astype(jnp.bfloat16)
        dkv_ref[heads*HD:, :] = dva_ref[...].astype(jnp.bfloat16)

def attend_back(counts, q_t, g_t, o_t, lse, k, v, bq=256, blocks=4):
    width, rows = q_t.shape
    nk = k.shape[0]
    heads = width//HD
    per = pl.BlockSpec((width,bq), lambda i,c:(0,i))
    whole = pl.BlockSpec((nk,width), lambda i,c:(0,0))
    wide = pl.BlockSpec((2*width,nk), lambda i,c:(0,0))
    return pl.pallas_call(
        functools.partial(attend_back_kernel, heads=heads, blocks=blocks),
        grid_spec=pltpu.PrefetchScalarGridSpec(
            num_scalar_prefetch=1, grid=(rows//bq,),
            in_specs=[per,per,per,pl.BlockSpec((8,bq), lambda i,c:(0,i)),whole,whole],
            out_specs=[per,wide],
            scratch_shapes=[pltpu.VMEM((width,nk), jnp.bfloat16),pltpu.VMEM((width,nk), jnp.float32),pltpu.VMEM((width,nk), jnp.float32)]),
        out_shape=(jax.ShapeDtypeStruct((width,rows),jnp.bfloat16),)+(jax.ShapeDtypeStruct((2*width,nk),jnp.bfloat16),),
        compiler_params=pltpu.CompilerParams(dimension_semantics=("arbitrary",), vmem_limit_bytes=48<<20),
        cost_estimate=pl.CostEstimate(flops=10*rows*nk*width*4, transcendentals=rows*nk*heads, bytes_accessed=16*rows*width),
        name="attend_back",
    )(counts, q_t, g_t, o_t, lse, k, v)


from jax.sharding import Mesh, PartitionSpec as P

D = 768
H = 12
FF = 3072
BLOCK = 256
norm_epsilon = 1e-05
root_half = 0.7071067811865476
density_factor = 0.3989422804014327
DP = ("outer", "mid", "core")
EVERY = ("outer", "mid", "core", "tensor")


def dot_tn(former, latter):
    return lax.dot_general(former, latter, (((0,), (0,)), ((), ())), preferred_element_type=jnp.float32)


def dot_tt(former, latter):
    return lax.dot_general(former, latter, (((0,), (1,)), ((), ())), preferred_element_type=jnp.float32)


def normed_of(summed):
    centered = summed - jnp.mean(summed, axis=-1, keepdims=True)
    inverse = lax.rsqrt(jnp.mean(centered * centered, axis=-1, keepdims=True) + norm_epsilon)
    return centered * inverse, inverse


def layer_norm(summed, norm_gain, norm_shift):
    return normed_of(summed)[0] * norm_gain + norm_shift


def layer_norm_back(upstream, summed, norm_gain):
    normed, inverse = normed_of(summed)
    scaled = upstream * norm_gain
    through = inverse * (
        scaled
        - jnp.mean(scaled, axis=-1, keepdims=True)
        - normed * jnp.mean(scaled * normed, axis=-1, keepdims=True)
    )
    return (through, jnp.sum(upstream * normed, axis=0), jnp.sum(upstream, axis=0))


def units_kernel(x_ref, up_ref, down_ref, bias_ref, active_ref, slope_ref, out_ref, acc_ref):
    i = pl.program_id(0)
    before = dot_nn(x_ref[...], up_ref[0]) + bias_ref[...]
    chance = 0.5 * (1.0 + lax.erf(before * root_half))
    active = (before * chance).astype(jnp.bfloat16)
    active_ref[...] = active
    slope_ref[...] = (chance + before * density_factor * jnp.exp(-0.5 * before * before)).astype(jnp.bfloat16)
    part = dot_nt(active, down_ref[0])

    @pl.when(i == 0)
    def _():
        acc_ref[...] = part

    @pl.when(i > 0)
    def _():
        acc_ref[...] += part

    @pl.when(i == pl.num_programs(0) - 1)
    def _():
        out_ref[...] = acc_ref[...]


def units(x, both, bias):
    rows, width = x.shape
    count = both.shape[0]
    local = both.shape[2] // 2
    cols = pl.BlockSpec((rows, local), lambda i: (0, i))
    return pl.pallas_call(
        units_kernel,
        grid=(count,),
        in_specs=[pl.BlockSpec((rows, width), lambda i: (0, 0)),
                  pl.BlockSpec((1, width, local), lambda i: (i, 0, 0)),
                  pl.BlockSpec((1, width, local), lambda i: (i, 0, 1)),
                  pl.BlockSpec((1, local), lambda i: (0, i))],
        out_specs=[cols, cols, pl.BlockSpec((rows, width), lambda i: (0, 0))],
        scratch_shapes=[pltpu.VMEM((rows, width), jnp.float32)],
        out_shape=(jax.ShapeDtypeStruct((rows, count * local), jnp.bfloat16),) * 2
        + (jax.ShapeDtypeStruct((rows, width), jnp.float32),),
        compiler_params=pltpu.CompilerParams(dimension_semantics=("arbitrary",), vmem_limit_bytes=40 << 20),
        name="units",
    )(x, both, both, bias)


def units_back_kernel(g_ref, up_ref, down_ref, slope_ref, grad_ref, sums_ref, out_ref, acc_ref):
    i = pl.program_id(0)
    grad = (dot_nn(g_ref[...], down_ref[0]) * slope_ref[...].astype(jnp.float32)).astype(jnp.bfloat16)
    grad_ref[...] = grad
    sums_ref[...] = jnp.sum(grad.astype(jnp.float32), axis=0, keepdims=True)
    part = dot_nt(grad, up_ref[0])

    @pl.when(i == 0)
    def _():
        acc_ref[...] = part

    @pl.when(i > 0)
    def _():
        acc_ref[...] += part

    @pl.when(i == pl.num_programs(0) - 1)
    def _():
        out_ref[...] = acc_ref[...]


def units_back(g, both, slope):
    rows, width = g.shape
    count = both.shape[0]
    local = both.shape[2] // 2
    cols = pl.BlockSpec((rows, local), lambda i: (0, i))
    return pl.pallas_call(
        units_back_kernel,
        grid=(count,),
        in_specs=[pl.BlockSpec((rows, width), lambda i: (0, 0)),
                  pl.BlockSpec((1, width, local), lambda i: (i, 0, 0)),
                  pl.BlockSpec((1, width, local), lambda i: (i, 0, 1)),
                  cols],
        out_specs=[cols, pl.BlockSpec((1, local), lambda i: (0, i)), pl.BlockSpec((rows, width), lambda i: (0, 0))],
        scratch_shapes=[pltpu.VMEM((rows, width), jnp.float32)],
        out_shape=(jax.ShapeDtypeStruct((rows, count * local), jnp.bfloat16),
                   jax.ShapeDtypeStruct((1, count * local), jnp.float32),
                   jax.ShapeDtypeStruct((rows, width), jnp.float32)),
        compiler_params=pltpu.CompilerParams(dimension_semantics=("arbitrary",), vmem_limit_bytes=40 << 20),
        name="units_back",
    )(g, both, both, slope)


COLUMN = ("core", "tensor")


def place_of(sequence, quarter):
    return (quarter // 2) * 4 + 2 * sequence + quarter % 2


def relocated(x):
    return lax.ppermute(x, COLUMN, [(s * 4 + t, place_of(s, t)) for s in range(2) for t in range(4)])


def group_swapped(x, delta):
    return lax.ppermute(x, COLUMN, [(place_of(s, q), place_of(s, q ^ delta)) for s in range(2) for q in range(4)])


def quarter_rank():
    return 2 * lax.axis_index("core") + lax.axis_index("tensor") % 2


def half_rank():
    return lax.axis_index("tensor") // 2


def swapped(x, axis):
    return lax.ppermute(x, axis, [(0, 1), (1, 0)])


def ordered(x, other, rank, dim=0):
    place = lax.broadcasted_iota(jnp.int32, (1,) * dim + (2,) + (1,) * (x.ndim - dim), dim)
    return jnp.where(place == rank, jnp.expand_dims(x, dim), jnp.expand_dims(other, dim))


def gather_axis(x, axis, dim=0):
    if lax.axis_size(axis) != 2:
        return lax.all_gather(x, axis, axis=dim)
    return ordered(x, swapped(x, axis), lax.axis_index(axis), dim)


def piece_of(x, index, size, dim):
    return lax.dynamic_slice_in_dim(x, index * size, size, dim)


def group_exchange(x, size, dim, out_dim, out_size):
    rank = quarter_rank()
    shape = list(x.shape)
    shape[dim] = size
    shape[out_dim] = 4 * out_size
    got = [(group_swapped(piece_of(x, rank ^ d, size, dim), d), rank ^ d) for d in (3, 1, 2)]
    out = jnp.zeros(tuple(shape), x.dtype)
    for piece, source in [(piece_of(x, rank, size, dim), rank)] + got[::-1]:
        out = lax.dynamic_update_slice_in_dim(out, piece, source * out_size, out_dim)
    return out


def tokens_to_heads(whole):
    return group_exchange(whole, whole.shape[0] // 4, 0, 1, whole.shape[1])


def heads_to_tokens(mine):
    return group_exchange(mine, mine.shape[1] // 4, 1, 0, mine.shape[0])


def gather_quarters(mine):
    pair = ordered(mine, group_swapped(mine, 1), lax.axis_index("tensor") % 2)
    whole = ordered(pair, group_swapped(pair, 2), lax.axis_index("core"))
    return whole.reshape((-1,) + mine.shape[1:])


def added(a, b):
    return a.astype(jnp.float32) + b.astype(jnp.float32)


def parts_of(x, rank, dim=0):
    return (lax.dynamic_index_in_dim(x, rank, dim, keepdims=False),
            lax.dynamic_index_in_dim(x, 1 - rank, dim, keepdims=False))


def scatter_quarters(partial):
    whole = partial.reshape((2, 2, -1) + partial.shape[1:])
    keep, send = parts_of(whole, lax.axis_index("core"))
    got = group_swapped(send, 2)
    low = lax.axis_index("tensor") % 2
    keep, send = [added(a, b) for a, b in zip(parts_of(keep, low), parts_of(got, low))]
    return keep + group_swapped(send.astype(jnp.bfloat16), 1).astype(jnp.float32)


def gather_shards(x):
    count = lax.axis_size("tensor")
    rank = lax.axis_index("tensor")
    out = jnp.zeros((count,) + x.shape, x.dtype)
    got = [(lax.ppermute(x, "tensor", [(i, (i + s) % count) for i in range(count)]), (rank - s) % count)
           for s in range(1, count)]
    for piece, source in [(x, rank)] + got:
        out = lax.dynamic_update_slice_in_dim(out, piece[None], source, 0)
    return out


def column_sums(partial):
    count = lax.axis_size("tensor")
    rank = lax.axis_index("tensor")
    width = partial.shape[1] // count
    total = piece_of(partial, rank, width, 1).astype(jnp.float32)
    for s in range(1, count):
        piece = piece_of(partial, (rank + s) % count, width, 1)
        total = total + lax.ppermute(
            piece, "tensor", [(i, (i + s) % count) for i in range(count)]).astype(jnp.float32)
    return total


def interleaved(parts):
    count = lax.axis_size("tensor")
    rows = parts[0].shape[0]
    return jnp.concatenate([p.reshape(rows, count, -1) for p in parts], axis=2).reshape(rows, -1)


def summed_everywhere(x):
    for axis in DP:
        if lax.axis_size(axis) == 2:
            x = x + swapped(x, axis)
        else:
            x = lax.psum(x, axis)
    count = lax.axis_size("tensor")
    for d in (1, 2):
        x = x + lax.ppermute(x, "tensor", [(i, i ^ d) for i in range(count)])
    return x


def tied(*values):
    return lax.optimization_barrier(values)


def paired():
    return lax.axis_size("outer") == 2


def reduce_rows(partial):
    return lax.psum_scatter(partial, DP, scatter_dimension=0, tiled=True)


def outer_scatter(partial, count):
    return lax.psum_scatter(partial, "outer", scatter_dimension=0, tiled=True)


class Flow:
    def __init__(self, kept, got, axes):
        self.axes = list(axes) if paired() else ["outer", "mid"]
        lead = (lax.axis_size("outer"), 2, -1) + kept.shape[1:]
        self.kept = kept.reshape(lead)
        self.moving = None if got is None else got.reshape(lead)

    def across(self):
        axis = self.axes.pop(0)
        low = jnp.bfloat16
        if lax.axis_size(axis) != 2:
            whole = self.kept if self.moving is None else added(self.kept, self.moving).astype(low)
            self.kept = lax.psum_scatter(whole, axis, scatter_dimension=0, tiled=False)
            self.moving = None
            return
        dim = 1 if axis == "mid" and self.axes else 0
        rank = lax.axis_index(axis)
        if self.moving is None:
            keep, send = parts_of(self.kept, rank, dim)
        else:
            keep, send = [added(a, b).astype(low) for a, b in zip(
                parts_of(self.kept, rank, dim), parts_of(self.moving, rank, dim))]
        self.kept, self.moving = keep, swapped(send, axis)

    def total(self):
        if self.moving is None:
            return self.kept
        return added(self.kept, self.moving).astype(jnp.bfloat16)


def core_halves(former, latter):
    rows = former.shape[1] // lax.axis_size(DP)
    halves = parts_of(former.reshape(former.shape[0], -1, 2, rows), lax.axis_index("core"), 2)
    return [dot_tn(h.reshape(former.shape[0], -1), latter).astype(jnp.bfloat16) for h in halves]


def shard_total(summed):
    rank = half_rank()
    keep, send = parts_of(summed.reshape(2, -1, summed.shape[-1]), rank)
    got = lax.ppermute(send, "tensor", [(i, i ^ 2) for i in range(4)])
    return relocated(added(keep, got).astype(jnp.bfloat16)).astype(jnp.float32)


def body(
    inputs,
    encoder_out,
    block_ids,
    out_grad,
    in_weight,
    out_weight,
    up_weight,
    down_weight,
    vectors,
    norm_gains,
    up_bias,
):
    low = jnp.bfloat16
    count = lax.axis_size("tensor")
    width = D // count
    scale = HD ** (-0.5)
    quarter = quarter_rank()
    start = quarter * width
    core = lax.axis_index("core")

    in_low = in_weight.astype(low)
    shards = in_low.shape[1]
    rows = relocated(inputs[0])
    qkv_all = gather_shards(jnp.concatenate([in_low[0], in_low[1], in_low[2]], axis=1))
    hidden_self = gather_quarters(rows)

    def own_shard(stacked):
        mine = lax.dynamic_index_in_dim(stacked, quarter, 0, keepdims=False)
        theirs = lax.dynamic_index_in_dim(stacked, quarter ^ 2, 0, keepdims=False)
        return ordered(mine, swapped(theirs, "core"), core)

    w_self = gather_axis(gather_axis(own_shard(qkv_all), "mid"), "outer").reshape(D, 3 * width)
    unit_pack = jnp.concatenate([up_weight.astype(low), down_weight.astype(low).T], axis=1)
    unit_pack = lax.all_gather(unit_pack, ("tensor",) + DP, axis=0, tiled=True).reshape(count, D, -1)
    out_turned = jnp.swapaxes(out_weight.astype(low), 1, 2)
    mid_all = jnp.concatenate([in_low[4], in_low[5], in_low[3], out_turned[0], out_turned[1]], axis=1)
    encoder, mid_all, hidden_self = tied(encoder_out[0], mid_all, hidden_self)
    mid_all = gather_shards(mid_all)
    encoder = relocated(encoder)
    kv_mine = own_shard(mid_all[:, :, : 2 * width])
    full = jnp.transpose(mid_all[:, :, 2 * width :].reshape(count, shards, 3, width), (1, 2, 0, 3))
    pack = jnp.concatenate([kv_mine[0], kv_mine[1], full.reshape(shards, 3 * D)], axis=1)
    pack = gather_axis(gather_axis(pack, "mid"), "outer")
    encoder_full = gather_quarters(encoder)

    ids = block_ids[0]
    ids = jnp.where(core == half_rank(), ids, swapped(ids, "core"))
    head_bias = lax.dynamic_slice_in_dim(vectors[0:4], start, width, 1)
    counts_self = jnp.sum((ids[None, :] <= ids[:, None]).astype(jnp.int32), axis=1)
    counts_cross = jnp.full((ids.shape[0] // 2,), 4 * encoder.shape[0] // KB, jnp.int32)

    q_self = ((dot_tt(w_self[:, :width], hidden_self) + head_bias[0][:, None]) * scale).astype(low)
    k_self = dot_nn(hidden_self, w_self[:, width : 2 * width]).astype(low)
    v_self = (dot_nn(hidden_self, w_self[:, 2 * width :]) + head_bias[1]).astype(low)
    mine_self, lse_self = attend(counts_self, q_self, k_self, v_self)
    mixed_self = heads_to_tokens(mine_self)
    mine_self, pack, encoder_full = tied(mine_self, pack, encoder_full)
    upstream = relocated(out_grad[0])
    w_cross = jnp.stack([pack[..., : 2 * width], pack[..., 2 * width : 4 * width]], axis=2).reshape(D, 2 * width)
    projections = gather_axis(pack[..., 4 * width :], "core", 2).reshape(D, 3 * D)
    wq_cross, wo_self, wo_cross = (projections[:, n * D : (n + 1) * D] for n in range(3))
    k_cross = dot_nn(encoder_full, w_cross[:, :width]).astype(low)
    v_cross = (dot_nn(encoder_full, w_cross[:, width:]) + head_bias[3]).astype(low)
    summed_one = rows.astype(jnp.float32) + (dot_tt(mixed_self, wo_self) + vectors[4])
    normed_one = layer_norm(summed_one, norm_gains[0], vectors[7])
    hidden_cross = normed_one.astype(low)
    q_cross = tokens_to_heads(((dot_tt(wq_cross, hidden_cross) + vectors[2][:, None]) * scale).astype(low))
    mine_cross, lse_cross = attend(counts_cross, q_cross, k_cross, v_cross, bq=512)
    mixed_cross = heads_to_tokens(mine_cross)
    summed_two = normed_one + (dot_tt(mixed_cross, wo_cross) + vectors[5])
    normed_two = layer_norm(summed_two, norm_gains[1], vectors[8])
    hidden_units = normed_two.astype(low)
    active, slope, unit_out = units(hidden_units, unit_pack, up_bias[None])
    summed_three = normed_two + (unit_out + vectors[6])
    layer_out = layer_norm(summed_three, norm_gains[2], vectors[9]).astype(low)

    grad_three, gain_three, shift_three = layer_norm_back(upstream.astype(jnp.float32), summed_three, norm_gains[2])
    branch_three = grad_three.astype(low)
    bias_down = jnp.sum(branch_three.astype(jnp.float32), axis=0)
    grad_before, unit_bias, unit_back = units_back(branch_three, unit_pack, slope)
    grad_two, gain_two, shift_two = layer_norm_back(grad_three + unit_back, summed_two, norm_gains[1])
    branch_two = grad_two.astype(low)
    bias_cross_out = jnp.sum(branch_two.astype(jnp.float32), axis=0)
    grad_mixed_cross = tokens_to_heads(dot_tt(wo_cross, branch_two).astype(low))
    down_kept, down_sent = core_halves(branch_three, active)
    up_kept, up_sent = core_halves(hidden_units, grad_before)
    grad_mixed_cross, down_kept, down_sent, up_kept, up_sent = tied(
        grad_mixed_cross, down_kept, down_sent, up_kept, up_sent)
    down_got, up_got = swapped(down_sent, "core"), swapped(up_sent, "core")
    layer_out = relocated(layer_out)
    dq_mine, dkv_cross = attend_back(
        counts_cross, q_cross, grad_mixed_cross, mine_cross, lse_cross, k_cross, v_cross, bq=512)
    dq_mine, dkv_cross, down_got, up_got, layer_out = tied(dq_mine, dkv_cross, down_got, up_got, layer_out)
    dq_cross = heads_to_tokens(dq_mine)
    down = Flow(down_kept, down_got, ("mid", "outer"))
    up = Flow(up_kept, up_got, ("outer", "mid"))
    down.across()
    up.across()
    encoder_part = dot_tt(dkv_cross, w_cross).astype(low)
    kv_flow = Flow(dot_tt(encoder_full, dkv_cross).astype(low), None, ("mid", "outer"))
    out_grad_cross = dot_tt(branch_two, mixed_cross).astype(low)
    bias_query_cross = jnp.sum(dq_cross.astype(jnp.float32), axis=1)
    bias_value_cross = jnp.sum(dkv_cross[width:].astype(jnp.float32), axis=1)
    grad_one_in = grad_two + dot_tt(dq_cross, wq_cross)
    grad_one, gain_one, shift_one = layer_norm_back(grad_one_in, summed_one, norm_gains[0])
    branch_one = grad_one.astype(low)
    bias_self_out = jnp.sum(branch_one.astype(jnp.float32), axis=0)
    grad_mixed_self = tokens_to_heads(dot_tt(wo_self, branch_one).astype(low))
    query_grad_cross = dot_tt(hidden_cross, dq_cross).astype(low)
    out_grad_self = dot_tt(branch_one, mixed_self).astype(low)
    square_grads = reduce_rows(jnp.concatenate([query_grad_cross, out_grad_self, out_grad_cross], axis=1))
    grad_mixed_self, down.moving, up.moving, query_grad_cross, out_grad_self, encoder_part = tied(
        grad_mixed_self, down.moving, up.moving, query_grad_cross, out_grad_self, encoder_part)
    down.across()
    up.across()
    kv_flow.across()
    encoder_sum = scatter_quarters(encoder_part)
    dq_self, dkv_self = attend_back(
        counts_self, q_self, grad_mixed_self, mine_self, lse_self, k_self, v_self)
    dq_self, dkv_self, down.moving, up.moving, kv_flow.moving, encoder_sum = tied(
        dq_self, dkv_self, down.moving, up.moving, kv_flow.moving, encoder_sum)
    dqkv = jnp.concatenate([dq_self, dkv_self], axis=0)
    input_part = dot_tt(dqkv, w_self).astype(low)
    input_part, dqkv = tied(input_part, dqkv)
    input_sum = grad_one + scatter_quarters(input_part)
    input_grad = relocated(input_sum.astype(low)).astype(jnp.float32)
    self_flow = Flow(dot_tt(hidden_self, dqkv).astype(low), None, ("outer", "mid"))
    self_flow.across()
    kv_flow.across()
    self_flow.across()
    head_grads = shard_total(jnp.concatenate([
        t.reshape(-1, t.shape[-1]) for t in (self_flow.total(), kv_flow.total())], axis=1))
    encoder_grad = relocated(encoder_sum.astype(low)).astype(jnp.float32)
    bias_query_self = jnp.sum(dq_self.astype(jnp.float32), axis=1)
    bias_value_self = jnp.sum(dkv_self[width:].astype(jnp.float32), axis=1)

    unit_sums = column_sums(interleaved([t.reshape(shards, -1) for t in (up.total(), down.total())]))
    units_here = unit_sums.shape[1] // 2
    square_sums = column_sums(interleaved([square_grads[:, n * D : (n + 1) * D] for n in range(3)]))
    head = [head_grads[:, n * width : (n + 1) * width] for n in range(5)]
    in_shard = jnp.stack([head[0], head[1], head[2], square_sums[:, :width], head[3], head[4]])
    out_shard = jnp.stack([square_sums[:, width : 2 * width].T, square_sums[:, 2 * width :].T])

    def embed(part):
        return lax.dynamic_update_slice_in_dim(jnp.zeros((D,), jnp.float32), part, start, 0)

    small = jnp.stack([
        embed(bias_query_self), embed(bias_value_self), bias_query_cross, embed(bias_value_cross),
        bias_self_out, bias_cross_out, bias_down, shift_one, shift_two, shift_three,
        gain_one, gain_two, gain_three])
    small = summed_everywhere(jnp.concatenate([small, unit_bias.reshape(-1, D)], axis=0))
    return (
        layer_out[None],
        input_grad[None],
        encoder_grad[None],
        in_shard,
        out_shard,
        unit_sums[:, :units_here],
        unit_sums[:, units_here:].T,
        small[:10],
        small[10:13],
        small[13:].reshape(-1),
    )


def solution(mesh):
    devices = mesh.devices
    wide = Mesh(devices.reshape(devices.shape[0] // 4, 2, 2, devices.shape[1]), EVERY)
    return jax.shard_map(
        body,
        mesh=wide,
        in_specs=(
            P(DP, "tensor", None),
            P(DP, "tensor", None),
            P(DP, None),
            P(DP, "tensor", None),
            P(None, DP, "tensor"),
            P(None, "tensor", DP),
            P(DP, "tensor"),
            P("tensor", DP),
            P(),
            P(),
            P(),
        ),
        out_specs=(
            P(DP, "tensor", None),
            P(DP, "tensor", None),
            P(DP, "tensor", None),
            P(None, DP, "tensor"),
            P(None, "tensor", DP),
            P(DP, "tensor"),
            P("tensor", DP),
            P(),
            P(),
            P(),
        ),
        check_vma=False,
    )
```
